32 devices in a mesh: dp: 4 (over y, x), tp: 8 (over z, core).
Axes of the slice: x: 2, y: 2, z: 4, core: 2. Of those that a mesh axis runs over, the one named last changes fastest.
Arguments:
- tokens: bfloat16 [4, 2048, 2048], P('dp', 'tp'), may hold values from -6 to 6
- doc_ids: int32 [4, 2048], P('dp', 'tp'), may hold values from 0 to 7, never falling along the last dimension, each value on 1 to 512 neighbouring positions
- fill: int32 [4], P('dp'), may hold values from 1024 to 2048
- gain_attn: float32 [2048], replicated, may hold values from 0.5 to 1.5
- w_query: bfloat16 [2048, 256], replicated, may hold values from -0.1875 to 0.1875
- w_key: bfloat16 [2048, 256], replicated, may hold values from -0.1875 to 0.1875
- w_value: bfloat16 [2048, 2048], replicated, may hold values from -0.125 to 0.125
- w_out: bfloat16 [2048, 2048], replicated, may hold values from -1 to 1
- gain_mlp: float32 [2048], replicated, may hold values from 0.5 to 1.5
- w_gate_up: bfloat16 [2, 2048, 5632], P(None, None, 'tp'), may hold values from -0.125 to 0.125
- w_down: bfloat16 [5632, 2048], P('tp'), may hold values from -0.078125 to 0.078125
- out_grad: bfloat16 [4, 2048, 2048], P('dp', 'tp'), may hold values from -6 to 6
Outputs:
- output: bfloat16 [4, 2048, 2048], P('dp', 'tp')
- input_grad: float32 [4, 2048, 2048], P('dp', 'tp')
- gain_attn_grad: float32 [2048], P(('dp', 'tp'))
- w_query_grad: float32 [2048, 256], P(('dp', 'tp'))
- w_key_grad: float32 [2048, 256], P(('dp', 'tp'))
- w_value_grad: float32 [2048, 2048], P(('dp', 'tp'))
- w_out_grad: float32 [2048, 2048], P(('dp', 'tp'))
- gain_mlp_grad: float32 [2048], P(('dp', 'tp'))
- w_gate_up_grad: float32 [2, 2048, 5632], P(None, None, 'tp')
- w_down_grad: float32 [5632, 2048], P('tp')
The draws below stay inside these ranges and needn't reach their ends.
Inputs may be any that keep to these rules, and one draw needn't show every extreme that they name: `doc_ids`: within a sequence the ids never fall; each of the 8 documents holds 1 to 512 tokens.
All inputs are finite; a program needn't handle non-finite values.
Results may differ from the reference program's by a relative error of at most 0.039.
Values may be sent and summed in bfloat16 or wider, within the bound.
A program may use at most 640 MiB of HBM per device.

```python
import math
import jax
import jax.numpy as jnp
import numpy as np
from jax import lax

D = 2048
FF = 5632
HEADS = 16
FEAT = 16
LENGTH = 2048
SEGS = 8
SEQUENCES = 4


def place_ends(result, key, low, largest):
    index_at = [jax.random.randint(jax.random.fold_in(key, axis), (), 0, length) for axis, length in enumerate(result.shape)]
    widest = result.shape.index(max(result.shape))
    beside = index_at[:widest] + [(index_at[widest] + 1) % result.shape[widest]] + index_at[widest + 1:]
    return result.at[tuple(index_at)].set(low).at[tuple(beside)].set(largest)


def block_levels(rng, shape, cuts, least, largest):
    factor_of, own = 1.0, jax.random.fold_in(rng, 6)
    for axis_at, shards_of in cuts:
        heights = jnp.exp(jax.random.uniform(jax.random.fold_in(own, axis_at), (shards_of,), jnp.float32, least / len(cuts), largest / len(cuts)))
        factor_of = factor_of * jnp.repeat(heights, shape[axis_at] // shards_of).reshape([-1 if axis == axis_at else 1 for axis in range(len(shape))])
    return factor_of


def split_up(amount, total, bound, slope):
    loads = [(1 << 20) // math.isqrt(standing ** slope) + 1 for standing in range(2, amount + 1)]
    surplus, holding = total - bound - (amount - 1), [1] * (amount - 1)
    while surplus > 0:
        candidates = [i for i in range(amount - 1) if holding[i] < bound]
        whole, left = sum([loads[i] for i in candidates]), surplus
        for i in candidates:
            extra = min(bound - holding[i], max(1, left * loads[i] // whole), surplus)
            holding[i] = holding[i] + extra
            surplus = surplus - extra
    return np.array([bound] + holding)


def uneven(key, amount, total, bound, slope):
    if amount == 2:
        one = jax.random.randint(key, (), max(1, total - bound), min(bound, total - 1) + 1)
        return jnp.stack([one, total - one])
    lengths = jnp.asarray(split_up(amount, total, bound, slope), jnp.int32)
    twos = (amount - 1) // 2
    source_of, sink = lengths[1:1 + 2 * twos:2], lengths[2:2 + 2 * twos:2]
    slack = jnp.minimum(source_of - 1, bound - sink)
    shifted = jax.random.randint(jax.random.fold_in(key, 1), (twos,), 0, 1 << 20) % (slack + 1)
    lengths = lengths.at[1:1 + 2 * twos:2].set(source_of - shifted).at[2:2 + 2 * twos:2].set(sink + shifted)
    return lengths[jax.random.permutation(jax.random.fold_in(key, 2), amount)]


def centred(rng, dims, width, reach, split=(), kind=jnp.bfloat16):
    result = width * jax.random.normal(rng, dims, jnp.float32)
    if split:
        result = result * block_levels(rng, dims, split, -0.22, 0.18)
    return jnp.clip(result, -reach, reach).astype(kind)


def setup_inputs(seed: int = 0) -> dict:
    key_list = jax.random.split(jax.random.key(seed), 13)
    return {
        "tokens": centred(key_list[0], (SEQUENCES, LENGTH, D), 1.0, 6.0, ((0, 4), (1, 8))),
        "doc_ids": jax.vmap(lambda own: jnp.searchsorted(jnp.cumsum(uneven(own, SEGS, LENGTH, LENGTH // 4, 1)), jnp.arange(LENGTH), side="right"))(jax.random.split(key_list[1], SEQUENCES)).reshape((SEQUENCES, LENGTH)).astype(jnp.int32),
        "fill": place_ends(jax.random.randint(key_list[2], (SEQUENCES,), LENGTH // 2, LENGTH + 1), jax.random.fold_in(key_list[2], 1), LENGTH // 2, LENGTH).astype(jnp.int32),
        "gain_attn": jnp.clip(1.0 + 0.1 * jax.random.normal(key_list[3], (D,), jnp.float32), 0.5, 1.5),
        "w_query": centred(key_list[4], (D, HEADS * FEAT), (D // 2) ** -0.5, 0.1875),
        "w_key": centred(key_list[5], (D, HEADS * FEAT), (D // 2) ** -0.5, 0.1875),
        "w_value": centred(key_list[6], (D, D), D ** -0.5, 0.125),
        "w_out": centred(key_list[7], (D, D), (D // 64) ** -0.5, 1.0),
        "gain_mlp": jnp.clip(1.0 + 0.1 * jax.random.normal(key_list[8], (D,), jnp.float32), 0.5, 1.5),
        "w_gate_up": centred(key_list[9], (2, D, FF), D ** -0.5, 0.125, ((2, 8),)),
        "w_down": centred(key_list[10], (FF, D), FF ** -0.5, 0.078125, ((0, 8),)),
        "out_grad": centred(key_list[11], (SEQUENCES, LENGTH, D), 1.0, 6.0, ((0, 4), (1, 8))),
    }


@jax.custom_vjp
def low(v):
    return lax.optimization_barrier(v.astype(jnp.bfloat16)).astype(jnp.float32)

@jax.custom_vjp
def low_back(v):
    return v

def low_keep(v):
    return (low(v), None)

def low_pass(kept, grad):
    return (grad,)

def back_keep(v):
    return (v, None)

def back_low(kept, grad):
    return (low(grad),)
low.defvjp(low_keep, low_pass)
low_back.defvjp(back_keep, back_low)
eps = 1e-05

def matmul(left, right):
    return jnp.dot(left, right, precision=lax.Precision.HIGHEST, preferred_element_type=jnp.float32)

def rms_scale(values, gain_vec):
    return values * lax.rsqrt(lax.optimization_barrier(jnp.mean(values * values, axis=-1, keepdims=True)) + eps) * gain_vec

def attend(queries, key_feats, values, labels):
    length = queries.shape[0]
    block_rows = min(512, length)
    columns = jnp.arange(length).astype(jnp.int32)

    def one_block(offset):
        part_q = lax.dynamic_slice_in_dim(queries, offset, block_rows, 0)
        part_labels = lax.dynamic_slice_in_dim(labels, offset, block_rows, 0)
        places = offset + jnp.arange(block_rows).astype(jnp.int32)
        scores = jnp.einsum('ihf,jhf->hij', part_q, key_feats, precision=lax.Precision.HIGHEST) * 0.25
        allowed = (columns[None, :] <= places[:, None]) & (part_labels[:, None] == labels[None, :])
        kernel = jnp.where(allowed[None], 1.0 + scores + 0.5 * scores * scores, 0.0)
        numerator = jnp.einsum('hij,jhe->ihe', kernel, values, precision=lax.Precision.HIGHEST)
        denominator = lax.optimization_barrier(jnp.sum(kernel, axis=2)).T
        return numerator / denominator[:, :, None]
    offsets = (jnp.arange(length // block_rows) * block_rows).astype(jnp.int32)
    blocks = lax.map(jax.checkpoint(one_block), offsets)
    return blocks.reshape(length, -1)

def layer(inputs, doc_row, fill_len, params):
    gain_attn, w_query, w_key, w_value, w_out, gain_mlp, w_gate_up, w_down = params
    length = inputs.shape[0]
    places = jnp.arange(length).astype(jnp.int32)
    labels = jnp.where(places < fill_len, doc_row, SEGS + places).astype(jnp.float32)
    first_in = low(rms_scale(inputs, gain_attn))
    queries = low(low_back(matmul(first_in, w_query))).reshape(length, HEADS, FEAT)
    key_feats = low(low_back(matmul(first_in, w_key))).reshape(length, HEADS, FEAT)
    values = low(low_back(matmul(first_in, w_value))).reshape(length, HEADS, D // HEADS)
    attended = attend(queries, key_feats, values, labels)
    residual = inputs + low_back(matmul(low(attended), w_out))
    second_in = low(rms_scale(residual, gain_mlp))
    gate = low_back(matmul(second_in, w_gate_up[0]))
    upward = low_back(matmul(second_in, w_gate_up[1]))
    hidden = low(jax.nn.silu(gate) * upward)
    return residual + matmul(hidden, w_down)

def reference(tokens, doc_ids, fill, gain_attn, w_query, w_key, w_value, w_out, gain_mlp, w_gate_up, w_down, out_grad):
    params = (gain_attn.astype(jnp.float32), w_query.astype(jnp.float32), w_key.astype(jnp.float32), w_value.astype(jnp.float32), w_out.astype(jnp.float32), gain_mlp.astype(jnp.float32), w_gate_up.astype(jnp.float32), w_down.astype(jnp.float32))

    def forward(inputs, weights):

        def one_seq(seq_item):
            return layer(seq_item[0], seq_item[1], seq_item[2], weights)
        return lax.map(jax.checkpoint(one_seq), (inputs, doc_ids, fill))
    output, pullback = jax.vjp(forward, tokens.astype(jnp.float32), params)
    input_grad, param_grads = pullback(out_grad.astype(jnp.float32))
    return (output.astype(jnp.bfloat16), input_grad, param_grads[0], param_grads[1], param_grads[2], param_grads[3], param_grads[4], param_grads[5], param_grads[6], param_grads[7])
```

```python
import functools

import jax
import jax.numpy as jnp
from jax import lax
from jax.experimental import pallas as pl
from jax.experimental.pallas import tpu as pltpu
from jax.sharding import PartitionSpec as P

HEADS = 16
FEAT = 16
SEGS = 8
DOC_MAX = 512
LANES = 128


eps = 1e-05
bf16 = jnp.bfloat16
f32 = jnp.float32


def norm_rows(values, gain_vec):
    inv_rms = lax.rsqrt(jnp.mean(values * values, axis=1, keepdims=True) + eps)
    return (values * inv_rms * gain_vec, inv_rms)


def norm_back(values, inv_rms, gain_vec, upstream):
    weighted = upstream * gain_vec
    inner_mean = jnp.mean(weighted * values, axis=1, keepdims=True)
    backward = inv_rms * (weighted - values * inv_rms * inv_rms * inner_mean)
    gain_grad = jnp.sum(upstream * values * inv_rms, axis=0)
    return (backward, gain_grad)


def shift(x, axis, by):
    n = lax.axis_size(axis)
    return lax.ppermute(x, axis, [(i, i + by) for i in range(n) if 0 <= i + by < n])


def swap(x, axis, bit):
    n = lax.axis_size(axis)
    return lax.ppermute(x, axis, [(i, i ^ (1 << bit)) for i in range(n)])


def bits_of(axis):
    return (lax.axis_size(axis) - 1).bit_length()


def side(axis, bit):
    return (lax.axis_index(axis) >> bit) & 1


def halve(x, axis, bit, dim):
    mine = side(axis, bit)
    keep = lax.dynamic_index_in_dim(x, mine, dim, False)
    give = lax.dynamic_index_in_dim(x, 1 - mine, dim, False)
    got = swap(give, axis, bit)
    return (keep.astype(f32) + got.astype(f32)).astype(x.dtype)


def scatter_sum(x, axis, dim, order):
    k = bits_of(axis)
    shape = x.shape
    x = x.reshape(shape[:dim] + (2,) * k + (shape[dim] >> k,) + shape[dim + 1 :])
    left = list(range(k))[::-1]
    for bit in order:
        at = left.index(bit)
        x = halve(x, axis, bit, dim + at)
        left.pop(at)
    return x


def gather_back(x, axis, dim, order):
    k = bits_of(axis)
    have = []
    for bit in order[::-1]:
        got = swap(x, axis, bit)
        mine = side(axis, bit)
        at = sum(1 for b in have if b > bit)
        low = jnp.where(mine == 0, x, got)
        high = jnp.where(mine == 0, got, x)
        x = jnp.stack([low, high], axis=dim + at)
        have.append(bit)
    shape = x.shape
    return x.reshape(shape[:dim] + (-1,) + shape[dim + k + 1 :])


def both_orders(axis):
    up = list(range(bits_of(axis)))
    return up, up[::-1]


def masks(row_label, key_labels, mask_ref, rows, blocks):
    at = lax.broadcasted_iota(jnp.int32, (rows, rows), 0)
    to = lax.broadcasted_iota(jnp.int32, (rows, rows), 1)
    for b in range(blocks):
        same = (row_label[...] == key_labels[b][...]) & (row_label[...] > 0.0)
        if b == 0:
            same = (same & (to <= at)) | (to == at)
        mask_ref[b] = jnp.where(same, 1.0, 0.0)


def lane_mask(head, shape):
    lanes = lax.broadcasted_iota(jnp.int32, shape, 1)
    return (lanes // FEAT) == head


def dot_t(a, b):
    return lax.dot_general(a, b, (((1,), (1,)), ((), ())), preferred_element_type=f32)


def dot_n(a, b):
    return lax.dot_general(a, b, (((1,), (0,)), ((), ())), preferred_element_type=f32)


def t_dot(a, b):
    return lax.dot_general(a, b, (((0,), (0,)), ((), ())), preferred_element_type=f32)


def attend_kernel(blocks, per, *refs):
    row_label, q_ref = refs[:2]
    key_labels, k_refs, v_refs = (refs[2 + i * blocks : 2 + (i + 1) * blocks] for i in range(3))
    a_ref, mask_ref = refs[2 + 3 * blocks :]
    rows = q_ref.shape[0]
    step = pl.program_id(0)

    @pl.when(step == 0)
    def _():
        masks(row_label, key_labels, mask_ref, rows, blocks)

    own = lane_mask(step % per, q_ref.shape)
    q = jnp.where(own, q_ref[...], jnp.zeros_like(q_ref[...]))
    num = jnp.zeros(v_refs[0].shape, f32)
    den = jnp.zeros((rows, 1), f32)
    for b in range(blocks):
        s = dot_t(q, k_refs[b][...]) * 0.25
        kappa = mask_ref[b] * (1.0 + s + 0.5 * s * s)
        den = den + jnp.sum(kappa, axis=1, keepdims=True)
        num = num + dot_n(kappa.astype(bf16), v_refs[b][...])
    a_ref[...] = (num / den).astype(a_ref.dtype)


def attend_back_kernel(blocks, per, *refs):
    row_label, q_ref, a_ref, dy_ref = refs[:4]
    key_labels, k_refs, v_refs = (refs[4 + i * blocks : 4 + (i + 1) * blocks] for i in range(3))
    outs = refs[4 + 3 * blocks :]
    dq_ref, dk_refs, dv_refs = outs[0], outs[1 : 1 + blocks], outs[1 + blocks : 1 + 2 * blocks]
    mask_ref, s_ref = outs[1 + 2 * blocks :]
    rows = q_ref.shape[0]
    step = pl.program_id(0)

    @pl.when(step == 0)
    def _():
        masks(row_label, key_labels, mask_ref, rows, blocks)

    @pl.when(step % per == 0)
    def _():
        dq_ref[...] = jnp.zeros_like(dq_ref)
        for ref in dk_refs:
            ref[...] = jnp.zeros_like(ref)

    own = lane_mask(step % per, q_ref.shape)
    q = jnp.where(own, q_ref[...], jnp.zeros_like(q_ref[...]))
    den = jnp.zeros((rows, 1), f32)
    for b in range(blocks):
        s = dot_t(q, k_refs[b][...]) * 0.25
        s_ref[b] = s
        den = den + jnp.sum(mask_ref[b] * (1.0 + s + 0.5 * s * s), axis=1, keepdims=True)
    dnum = (dy_ref[...] / den).astype(bf16)
    dden = -jnp.sum(dnum.astype(f32) * a_ref[...].astype(f32), axis=1, keepdims=True)
    dq = jnp.zeros(q_ref.shape, f32)
    for b in range(blocks):
        s = s_ref[b]
        mask = mask_ref[b]
        kappa = (mask * (1.0 + s + 0.5 * s * s)).astype(bf16)
        dv_refs[b][...] = t_dot(kappa, dnum).astype(dv_refs[b].dtype)
        dkappa = dot_t(dnum, v_refs[b][...]) + dden
        ds = (mask * dkappa * (0.25 + 0.25 * s)).astype(bf16)
        dq = dq + dot_n(ds, k_refs[b][...])
        dk_refs[b][...] += t_dot(ds, q)
    dq_ref[...] += jnp.where(own, dq, 0.0)


def attend_specs(rows, width, blocks):
    per = LANES // FEAT
    whole = lambda shape: pl.BlockSpec(shape, lambda h: (0, 0))
    feat = pl.BlockSpec((rows, LANES), lambda h: (0, h // per))
    wide = pl.BlockSpec((rows, width // HEADS), lambda h: (0, h))
    row, col = whole((rows, 1)), whole((1, rows))
    return per, row, col, feat, wide


def attend(row_label, q, key_labels, ks, vs):
    rows, width = vs[0].shape
    blocks = len(ks)
    per, row, col, feat, wide = attend_specs(rows, width, blocks)
    pairs = rows * rows * blocks * HEADS
    return pl.pallas_call(
        functools.partial(attend_kernel, blocks, per),
        out_shape=jax.ShapeDtypeStruct((rows, width), bf16),
        grid=(HEADS,),
        in_specs=[row, feat] + [col] * blocks + [feat] * blocks + [wide] * blocks,
        out_specs=wide,
        scratch_shapes=[pltpu.VMEM((blocks, rows, rows), f32)],
        cost_estimate=pl.CostEstimate(
            flops=4 * pairs * LANES, transcendentals=0, bytes_accessed=2 * rows * width * (blocks + 1)
        ),
        name="attend",
    )(row_label, q, *key_labels, *ks, *vs)


def attend_back(row_label, q, a, dy, key_labels, ks, vs):
    rows, width = vs[0].shape
    blocks = len(ks)
    per, row, col, feat, wide = attend_specs(rows, width, blocks)
    pairs = rows * rows * blocks * HEADS
    small = jax.ShapeDtypeStruct((rows, q.shape[1]), f32)
    big = [jax.ShapeDtypeStruct((rows, width), f32 if b == 0 else bf16) for b in range(blocks)]
    outs = pl.pallas_call(
        functools.partial(attend_back_kernel, blocks, per),
        out_shape=[small] * (1 + blocks) + big,
        grid=(HEADS,),
        in_specs=[row, feat, wide, wide] + [col] * blocks + [feat] * blocks + [wide] * blocks,
        out_specs=[feat] * (1 + blocks) + [wide] * blocks,
        scratch_shapes=[
            pltpu.VMEM((blocks, rows, rows), f32),
            pltpu.VMEM((blocks, rows, rows), f32),
        ],
        cost_estimate=pl.CostEstimate(
            flops=10 * pairs * LANES,
            transcendentals=0,
            bytes_accessed=2 * rows * width * (2 * blocks + 4),
        ),
        name="attend_back",
    )(row_label, q, a, dy, *key_labels, *ks, *vs)
    return outs[0], outs[1 : 1 + blocks], outs[1 + blocks :]


def window(x, hops):
    held = [x]
    for _ in range(hops):
        held.append(shift(held[-1], "tp", 1))
    return held


def window_sum(parts):
    total = parts[-1]
    for part in parts[-2::-1]:
        total = part.astype(f32) + shift(total.astype(bf16), "tp", -1).astype(f32)
    return total


def sum_over_dp(halves, dims):
    orders = both_orders("dp")
    done = []
    for i, (x, dim) in enumerate(zip(halves, dims)):
        order = orders[i % 2]
        done.append(gather_back(scatter_sum(x, "dp", dim, order), "dp", dim, order).astype(f32))
    return done


def scatter_rows(grad):
    columns = grad.shape[1]
    orders = both_orders("dp")
    cut = columns // 2
    halves = [
        scatter_sum(grad[:, i * cut : (i + 1) * cut], "dp", 0, orders[i]) for i in range(2)
    ]
    part = jnp.concatenate(halves, axis=1)
    return lax.psum_scatter(part, "tp", scatter_dimension=0, tiled=True).astype(f32)


def scatter_vectors(vectors):
    for axis in ("tp", "dp"):
        for bit in range(bits_of(axis)):
            vectors = vectors + swap(vectors, axis, bit)
    n = lax.axis_size("dp") * lax.axis_size("tp")
    at = lax.axis_index("dp") * lax.axis_size("tp") + lax.axis_index("tp")
    size = vectors.shape[1] // n
    return lax.dynamic_slice_in_dim(vectors, at * size, size, 1)


def local(
    tokens,
    doc_ids,
    fill,
    gain_attn,
    w_query,
    w_key,
    w_value,
    w_out,
    gain_mlp,
    w_gate_up,
    w_down,
    out_grad,
):
    seq_count, rows, width = tokens.shape
    hops = min(-(-(DOC_MAX - 1) // rows), lax.axis_size("tp") - 1)
    position = lax.axis_index("tp") * rows + jnp.arange(rows, dtype=jnp.int32)
    labels = jnp.where(position[None, :] < fill[:, None], doc_ids + 1, 0).astype(f32)
    key_labels = window(labels, hops)

    def of_seq(array, s):
        return array if seq_count == 1 else array[s * rows : (s + 1) * rows]

    def sight(s):
        return labels[s][:, None], [label[s : s + 1] for label in key_labels]

    def joined(parts):
        return parts[0] if seq_count == 1 else jnp.concatenate(parts, axis=0)

    upstream = out_grad.reshape(seq_count * rows, width)
    block_rows = lax.all_gather(upstream, "tp", axis=0, tiled=True)

    inputs = tokens.reshape(seq_count * rows, width).astype(f32)
    normed, inv_first = norm_rows(inputs, gain_attn)
    first_in = normed.astype(bf16)
    v = jnp.dot(first_in, w_value, preferred_element_type=f32).astype(bf16)
    vs = window(v, hops)
    k = jnp.dot(first_in, w_key, preferred_element_type=f32).astype(bf16)
    ks = window(k, hops)
    q = jnp.dot(first_in, w_query, preferred_element_type=f32).astype(bf16)
    mixed = []
    for s in range(seq_count):
        row_label, seen = sight(s)
        mixed.append(
            attend(row_label, of_seq(q, s), seen, [of_seq(x, s) for x in ks], [of_seq(x, s) for x in vs])
        )
    mixed_low = joined(mixed)
    residual = inputs + jnp.dot(mixed_low, w_out, preferred_element_type=f32)
    normed_two, inv_second = norm_rows(residual, gain_mlp)
    second_in, block_rows = lax.optimization_barrier((normed_two.astype(bf16), block_rows))

    all_second = lax.all_gather(second_in, "tp", axis=0, tiled=True)
    hidden_part = jnp.einsum("nd,fd->nf", block_rows, w_down, preferred_element_type=f32)
    gate_up = jnp.einsum("nd,cdf->ncf", all_second, w_gate_up, preferred_element_type=f32)
    gate, up = gate_up[:, 0], gate_up[:, 1]
    sigmoid_gate = jax.nn.sigmoid(gate)
    silu_gate = gate * sigmoid_gate
    silu_slope = sigmoid_gate * (1.0 + gate * (1.0 - sigmoid_gate))
    hidden = (silu_gate * up).astype(bf16)
    gate_up_grad = jnp.stack(
        [hidden_part * up * silu_slope, hidden_part * silu_gate], axis=1
    ).astype(bf16)
    norm_part = jnp.einsum(
        "ncf,cdf->nd", gate_up_grad, w_gate_up, preferred_element_type=f32
    ).astype(bf16)
    norm_grad = lax.psum_scatter(norm_part, "tp", scatter_dimension=0, tiled=True).astype(f32)

    hidden, gate_up_grad, _ = lax.optimization_barrier((hidden, gate_up_grad, norm_part))
    grad_down = jnp.einsum("nf,nd->fd", hidden, block_rows, preferred_element_type=f32).astype(bf16)
    grad_gate_up = jnp.einsum(
        "nd,ncf->cdf", all_second, gate_up_grad, preferred_element_type=f32
    ).astype(bf16)
    cut = width // 2
    reduced = sum_over_dp(
        [grad_down[:, :cut], grad_down[:, cut:], grad_gate_up[0], grad_gate_up[1]], [1, 1, 0, 0]
    )
    grad_down = jnp.concatenate(reduced[:2], axis=1)
    grad_gate_up = jnp.stack(reduced[2:])
    branch = lax.psum_scatter(
        jnp.dot(hidden, w_down, preferred_element_type=f32).astype(bf16),
        "tp",
        scatter_dimension=0,
        tiled=True,
    ).astype(f32)
    output = (residual + branch).astype(bf16).reshape(tokens.shape)

    back_two, grad_gain_mlp = norm_back(residual, inv_second, gain_mlp, norm_grad)
    resid_grad = upstream.astype(f32) + back_two
    out_low = resid_grad.astype(bf16)
    attended_grad = jnp.einsum("nd,kd->nk", out_low, w_out, preferred_element_type=f32)
    grad_w_out = scatter_rows(
        jnp.einsum("nk,nd->kd", mixed_low, out_low, preferred_element_type=f32).astype(bf16)
    )
    back = []
    for s in range(seq_count):
        row_label, seen = sight(s)
        back.append(
            attend_back(
                row_label,
                of_seq(q, s),
                of_seq(mixed_low, s),
                of_seq(attended_grad, s),
                seen,
                [of_seq(x, s) for x in ks],
                [of_seq(x, s) for x in vs],
            )
        )
    dq = joined([x[0] for x in back])
    dks = [joined([x[1][b] for x in back]) for b in range(hops + 1)]
    dvs = [joined([x[2][b] for x in back]) for b in range(hops + 1)]
    value_grad_low = window_sum(dvs).astype(bf16)
    key_grad_low = window_sum(dks).astype(bf16)
    query_grad_low = dq.astype(bf16)
    low = jnp.concatenate([value_grad_low, query_grad_low, key_grad_low], axis=1)
    grads = scatter_rows(
        jnp.einsum("nd,nk->dk", first_in, low, preferred_element_type=f32).astype(bf16)
    )
    narrow = w_query.shape[1]
    grad_w_value = grads[:, :width]
    grad_w_query = grads[:, width : width + narrow]
    grad_w_key = grads[:, width + narrow :]
    first_grad = jnp.einsum("nk,dk->nd", query_grad_low, w_query, preferred_element_type=f32)
    first_grad = first_grad + jnp.einsum(
        "nk,dk->nd", key_grad_low, w_key, preferred_element_type=f32
    )
    first_grad = first_grad + jnp.einsum(
        "nk,dk->nd", value_grad_low, w_value, preferred_element_type=f32
    )
    back_one, grad_gain_attn = norm_back(inputs, inv_first, gain_attn, first_grad)
    input_grad = (resid_grad + back_one).reshape(tokens.shape)
    gains = scatter_vectors(jnp.stack([grad_gain_attn, grad_gain_mlp]))
    return (
        output,
        input_grad,
        gains[0],
        grad_w_query,
        grad_w_key,
        grad_w_value,
        grad_w_out,
        gains[1],
        grad_gate_up,
        grad_down,
    )


def solution(mesh):
    placed = (
        P("dp", "tp", None),
        P("dp", "tp"),
        P("dp"),
        P(),
        P(),
        P(),
        P(),
        P(),
        P(),
        P(None, None, "tp"),
        P("tp", None),
        P("dp", "tp", None),
    )
    return jax.shard_map(
        local,
        mesh=mesh,
        in_specs=placed,
        out_specs=(
            P("dp", "tp", None),
            P("dp", "tp", None),
            P(("dp", "tp")),
            P(("dp", "tp"), None),
            P(("dp", "tp"), None),
            P(("dp", "tp"), None),
            P(("dp", "tp"), None),
            P(("dp", "tp")),
            P(None, None, "tp"),
            P("tp", None),
        ),
        check_vma=False,
    )
```

```python
import functools

import jax
import jax.numpy as jnp
from jax import lax
from jax.experimental import pallas as pl
from jax.experimental.pallas import tpu as pltpu
from jax.sharding import PartitionSpec as P

HEADS = 16
FEAT = 16
SEGS = 8
DOC_MAX = 512
LANES = 128


eps = 1e-05
bf16 = jnp.bfloat16
f32 = jnp.float32


def norm_rows(values, gain_vec):
    inv_rms = lax.rsqrt(jnp.mean(values * values, axis=1, keepdims=True) + eps)
    return (values * inv_rms * gain_vec, inv_rms)


def norm_back(values, inv_rms, gain_vec, upstream):
    weighted = upstream * gain_vec
    inner_mean = jnp.mean(weighted * values, axis=1, keepdims=True)
    backward = inv_rms * (weighted - values * inv_rms * inv_rms * inner_mean)
    gain_grad = jnp.sum(upstream * values * inv_rms, axis=0)
    return (backward, gain_grad)


def shift(x, axis, by):
    n = lax.axis_size(axis)
    return lax.ppermute(x, axis, [(i, i + by) for i in range(n) if 0 <= i + by < n])


def swap(x, axis, bit):
    n = lax.axis_size(axis)
    return lax.ppermute(x, axis, [(i, i ^ (1 << bit)) for i in range(n)])


def bits_of(axis):
    return (lax.axis_size(axis) - 1).bit_length()


def side(axis, bit):
    return (lax.axis_index(axis) >> bit) & 1


def halve(x, axis, bit, dim):
    mine = side(axis, bit)
    keep = lax.dynamic_index_in_dim(x, mine, dim, False)
    give = lax.dynamic_index_in_dim(x, 1 - mine, dim, False)
    got = swap(give, axis, bit)
    return (keep.astype(f32) + got.astype(f32)).astype(x.dtype)


def scatter_sum(x, axis, dim, order):
    k = bits_of(axis)
    shape = x.shape
    x = x.reshape(shape[:dim] + (2,) * k + (shape[dim] >> k,) + shape[dim + 1 :])
    left = list(range(k))[::-1]
    for bit in order:
        at = left.index(bit)
        x = halve(x, axis, bit, dim + at)
        left.pop(at)
    return x


def gather_back(x, axis, dim, order):
    k = bits_of(axis)
    have = []
    for bit in order[::-1]:
        got = swap(x, axis, bit)
        mine = side(axis, bit)
        at = sum(1 for b in have if b > bit)
        low = jnp.where(mine == 0, x, got)
        high = jnp.where(mine == 0, got, x)
        x = jnp.stack([low, high], axis=dim + at)
        have.append(bit)
    shape = x.shape
    return x.reshape(shape[:dim] + (-1,) + shape[dim + k + 1 :])


def both_orders(axis):
    up = list(range(bits_of(axis)))
    return up, up[::-1]


def masks(hot_refs, mask_ref, rows, blocks):
    at = lax.broadcasted_iota(jnp.int32, (rows, rows), 0)
    to = lax.broadcasted_iota(jnp.int32, (rows, rows), 1)
    for b in range(blocks):
        same = dot_t(hot_refs[0][...], hot_refs[b][...])
        if b == 0:
            same = jnp.where(to < at, same, jnp.where(to == at, 1.0, 0.0))
        mask_ref[b] = same


def lane_mask(head, shape):
    lanes = lax.broadcasted_iota(jnp.int32, shape, 1)
    return (lanes // FEAT) == head


def dot_t(a, b):
    return lax.dot_general(a, b, (((1,), (1,)), ((), ())), preferred_element_type=f32)


def dot_n(a, b):
    return lax.dot_general(a, b, (((1,), (0,)), ((), ())), preferred_element_type=f32)


def t_dot(a, b):
    return lax.dot_general(a, b, (((0,), (0,)), ((), ())), preferred_element_type=f32)


def attend_kernel(blocks, per, *refs):
    q_ref = refs[0]
    hot_refs, k_refs, v_refs = (refs[1 + i * blocks : 1 + (i + 1) * blocks] for i in range(3))
    a_ref, mask_ref = refs[1 + 3 * blocks :]
    rows = q_ref.shape[0]
    step = pl.program_id(0)

    @pl.when(step == 0)
    def _():
        masks(hot_refs, mask_ref, rows, blocks)

    own = lane_mask(step % per, q_ref.shape)
    q = jnp.where(own, q_ref[...], jnp.zeros_like(q_ref[...]))
    num = jnp.zeros(v_refs[0].shape, f32)
    den = jnp.zeros((rows, 1), f32)
    for b in range(blocks):
        s = dot_t(q, k_refs[b][...]) * 0.25
        kappa = mask_ref[b] * (1.0 + s + 0.5 * s * s)
        den = den + jnp.sum(kappa, axis=1, keepdims=True)
        num = num + dot_n(kappa.astype(bf16), v_refs[b][...])
    a_ref[...] = (num / den).astype(a_ref.dtype)


def attend_back_kernel(blocks, per, *refs):
    q_ref, a_ref, dy_ref = refs[:3]
    hot_refs, k_refs, v_refs = (refs[3 + i * blocks : 3 + (i + 1) * blocks] for i in range(3))
    outs = refs[3 + 3 * blocks :]
    dq_ref, dk_refs, dv_refs = outs[0], outs[1 : 1 + blocks], outs[1 + blocks : 1 + 2 * blocks]
    mask_ref, s_ref = outs[1 + 2 * blocks :]
    rows = q_ref.shape[0]
    step = pl.program_id(0)

    @pl.when(step == 0)
    def _():
        masks(hot_refs, mask_ref, rows, blocks)

    @pl.when(step % per == 0)
    def _():
        dq_ref[...] = jnp.zeros_like(dq_ref)
        for ref in dk_refs:
            ref[...] = jnp.zeros_like(ref)

    own = lane_mask(step % per, q_ref.shape)
    q = jnp.where(own, q_ref[...], jnp.zeros_like(q_ref[...]))
    den = jnp.zeros((rows, 1), f32)
    for b in range(blocks):
        s = dot_t(q, k_refs[b][...]) * 0.25
        s_ref[b] = s
        den = den + jnp.sum(mask_ref[b] * (1.0 + s + 0.5 * s * s), axis=1, keepdims=True)
    dnum = (dy_ref[...] / den).astype(bf16)
    dden = -jnp.sum(dnum.astype(f32) * a_ref[...].astype(f32), axis=1, keepdims=True)
    dq = jnp.zeros(q_ref.shape, f32)
    for b in range(blocks):
        s = s_ref[b]
        mask = mask_ref[b]
        kappa = (mask * (1.0 + s + 0.5 * s * s)).astype(bf16)
        dv_refs[b][...] = t_dot(kappa, dnum).astype(dv_refs[b].dtype)
        dkappa = dot_t(dnum, v_refs[b][...]) + dden
        ds = (mask * dkappa * (0.25 + 0.25 * s)).astype(bf16)
        dq = dq + dot_n(ds, k_refs[b][...])
        dk_refs[b][...] += t_dot(ds, q)
    dq_ref[...] += jnp.where(own, dq, 0.0)


def attend_specs(rows, width, narrow):
    per = LANES // FEAT
    assert width // HEADS == LANES and FEAT * HEADS == narrow
    feat = pl.BlockSpec((rows, LANES), lambda h: (0, h // per))
    wide = pl.BlockSpec((rows, LANES), lambda h: (0, h))
    key = pl.BlockSpec((rows, LANES), lambda h: (0, width // LANES + h // per))
    hot = pl.BlockSpec((rows, LANES), lambda h: (0, (width + narrow) // LANES))
    return per, feat, wide, key, hot


def attend(q, kvs):
    rows, narrow = q.shape
    width = kvs[0].shape[1] - narrow - LANES
    blocks = len(kvs)
    per, feat, wide, key, hot = attend_specs(rows, width, narrow)
    pairs = rows * rows * blocks * HEADS
    return pl.pallas_call(
        functools.partial(attend_kernel, blocks, per),
        out_shape=jax.ShapeDtypeStruct((rows, width), bf16),
        grid=(HEADS,),
        in_specs=[feat] + [hot] * blocks + [key] * blocks + [wide] * blocks,
        out_specs=wide,
        scratch_shapes=[pltpu.VMEM((blocks, rows, rows), f32)],
        cost_estimate=pl.CostEstimate(
            flops=4 * pairs * LANES, transcendentals=0, bytes_accessed=2 * rows * width * (blocks + 1)
        ),
        name="attend",
    )(q, *kvs, *kvs, *kvs)


def attend_back(q, a, dy, kvs):
    rows, narrow = q.shape
    width = a.shape[1]
    blocks = len(kvs)
    per, feat, wide, key, hot = attend_specs(rows, width, narrow)
    pairs = rows * rows * blocks * HEADS
    small = jax.ShapeDtypeStruct((rows, narrow), f32)
    big = [jax.ShapeDtypeStruct((rows, width), f32 if b == 0 else bf16) for b in range(blocks)]
    outs = pl.pallas_call(
        functools.partial(attend_back_kernel, blocks, per),
        out_shape=[small] * (1 + blocks) + big,
        grid=(HEADS,),
        in_specs=[feat, wide, wide] + [hot] * blocks + [key] * blocks + [wide] * blocks,
        out_specs=[feat] * (1 + blocks) + [wide] * blocks,
        scratch_shapes=[
            pltpu.VMEM((blocks, rows, rows), f32),
            pltpu.VMEM((blocks, rows, rows), f32),
        ],
        cost_estimate=pl.CostEstimate(
            flops=10 * pairs * LANES,
            transcendentals=0,
            bytes_accessed=2 * rows * width * (2 * blocks + 4),
        ),
        name="attend_back",
    )(q, a, dy, *kvs, *kvs, *kvs)
    return outs[0], outs[1 : 1 + blocks], outs[1 + blocks :]


def window(x, hops):
    held = [x]
    for _ in range(hops):
        held.append(shift(held[-1], "tp", 1))
    return held


def window_sum(parts):
    total = jnp.zeros_like(parts[-1])
    for part in parts[::-1]:
        total = (part.astype(f32) + total.astype(f32)).astype(bf16)
        total = shift(total, "tp", -1)
    return total.astype(f32)


def tie(value, *others):
    return lax.optimization_barrier((value,) + others)[0]


def pair_split(x):
    n = lax.axis_size("dp") * lax.axis_size("tp") // 2
    rows, width = x.shape
    x = x.reshape(rows, n, 2, width // (2 * n))
    mine = side("tp", 0)
    take = lambda at: lax.dynamic_index_in_dim(x, at, 2, False).reshape(rows, width // 2)
    return take(mine), take(1 - mine)


def x_t_y(x, y):
    return lax.dot_general(x, y, (((0,), (0,)), ((), ())), preferred_element_type=f32)


def rows_over_dp(part):
    cut = part.shape[1] // 2
    orders = both_orders("dp")
    return [scatter_sum(part[:, i * cut : (i + 1) * cut], "dp", 0, orders[i]) for i in range(2)]


def rows_over_chips(halves):
    n = lax.axis_size("tp")
    groups = [list(range(core, n, 2)) for core in range(2)]
    part = jnp.concatenate(halves, axis=1)
    return lax.psum_scatter(
        part, "tp", scatter_dimension=0, axis_index_groups=groups, tiled=True
    ).astype(f32)


class DpSum:
    def __init__(self, make, size, dim, order):
        self.make, self.size, self.dim, self.order = make, size, dim, order

    def begin(self):
        first = self.order[0]
        self.sent = swap(self.make(1 - side("dp", first)).astype(bf16), "dp", first)

    def keep(self):
        self.kept = self.make(side("dp", self.order[0])).astype(bf16)

    def fold(self):
        half = (self.kept.astype(f32) + self.sent.astype(f32)).astype(bf16)
        quarter = half.shape[self.dim] // 2
        mine = side("dp", self.order[1])
        cut = lambda at: lax.dynamic_slice_in_dim(half, at * quarter, quarter, self.dim)
        got = swap(cut(1 - mine), "dp", self.order[1])
        self.own = (cut(mine).astype(f32) + got.astype(f32)).astype(bf16)

    def back(self):
        self.near = swap(self.own, "dp", self.order[1])

    def back_more(self, *after):
        mine = side("dp", self.order[1])
        pick = lambda at: jnp.where(mine == at, self.own, self.near)
        self.half = jnp.concatenate([pick(0), pick(1)], axis=self.dim)
        self.half = tie(self.half, *after)
        self.far = swap(self.half, "dp", self.order[0])

    def end(self):
        mine = side("dp", self.order[0])
        pick = lambda at: jnp.where(mine == at, self.half, self.far).astype(f32)
        return [pick(0), pick(1)]


def scatter_vectors(vectors):
    for axis in ("tp", "dp"):
        for bit in range(bits_of(axis)):
            vectors = vectors + swap(vectors, axis, bit)
    n = lax.axis_size("dp") * lax.axis_size("tp")
    at = lax.axis_index("dp") * lax.axis_size("tp") + lax.axis_index("tp")
    size = vectors.shape[1] // n
    return lax.dynamic_slice_in_dim(vectors, at * size, size, 1)


def local(
    tokens,
    doc_ids,
    fill,
    gain_attn,
    w_query,
    w_key,
    w_value,
    w_out,
    gain_mlp,
    w_gate_up,
    w_down,
    out_grad,
):
    seq_count, rows, width = tokens.shape
    hops = min(-(-(DOC_MAX - 1) // rows), lax.axis_size("tp") - 1)
    position = lax.axis_index("tp") * rows + jnp.arange(rows, dtype=jnp.int32)
    labels = jnp.where(position[None, :] < fill[:, None], doc_ids + 1, 0).astype(f32)

    def of_seq(array, s):
        return array if seq_count == 1 else array[s * rows : (s + 1) * rows]

    def joined(parts):
        return parts[0] if seq_count == 1 else jnp.concatenate(parts, axis=0)

    upstream = out_grad.reshape(seq_count * rows, width)
    inputs = tokens.reshape(seq_count * rows, width).astype(f32)
    normed, inv_first = norm_rows(inputs, gain_attn)
    first_in = normed.astype(bf16)
    narrow = w_query.shape[1]
    v = jnp.dot(first_in, w_value, preferred_element_type=f32).astype(bf16)
    k = jnp.dot(first_in, w_key, preferred_element_type=f32).astype(bf16)
    marks = (labels.reshape(-1, 1) == 1.0 + jnp.arange(LANES, dtype=f32)[None, :]).astype(bf16)
    kvs = window(jnp.concatenate([v, k, marks], axis=1), hops)
    q = jnp.dot(first_in, w_query, preferred_element_type=f32).astype(bf16)
    block_rows = lax.all_gather(tie(upstream, kvs[-1]), "tp", axis=0, tiled=True)
    mixed_low = joined(
        [attend(of_seq(q, s), [of_seq(x, s) for x in kvs]) for s in range(seq_count)]
    )
    residual = inputs + jnp.dot(mixed_low, w_out, preferred_element_type=f32)
    normed_two, inv_second = norm_rows(residual, gain_mlp)
    second_in = normed_two.astype(bf16)
    mixed_mine, mixed_other = pair_split(mixed_low)
    first_mine, first_other = pair_split(first_in)

    all_second = lax.all_gather(tie(second_in, block_rows), "tp", axis=0, tiled=True)
    hidden_part = jnp.einsum("nd,fd->nf", block_rows, w_down, preferred_element_type=f32)
    all_second, hidden_part = lax.optimization_barrier((all_second, hidden_part))
    gate_up = jnp.einsum("nd,cdf->ncf", all_second, w_gate_up, preferred_element_type=f32)
    gate, up = gate_up[:, 0], gate_up[:, 1]
    sigmoid_gate = jax.nn.sigmoid(gate)
    silu_gate = gate * sigmoid_gate
    silu_slope = sigmoid_gate * (1.0 + gate * (1.0 - sigmoid_gate))
    hidden = (silu_gate * up).astype(bf16)
    gate_grad = (hidden_part * up * silu_slope).astype(bf16)
    up_grad = (hidden_part * silu_gate).astype(bf16)
    norm_part = (dot_t(gate_grad, w_gate_up[0]) + dot_t(up_grad, w_gate_up[1])).astype(bf16)
    norm_grad = lax.psum_scatter(norm_part, "tp", scatter_dimension=0, tiled=True)

    hidden, gate_grad, up_grad, _ = lax.optimization_barrier(
        (hidden, gate_grad, up_grad, norm_part)
    )
    orders = both_orders("dp")
    cut = width // 2

    def down_half(i):
        size = cut // 2
        return lambda at: x_t_y(
            hidden, lax.dynamic_slice_in_dim(block_rows, i * cut + at * size, size, 1)
        )

    def up_half(grad):
        return lambda at: x_t_y(lax.dynamic_slice_in_dim(all_second, at * cut, cut, 1), grad)

    sums = [DpSum(down_half(i), cut, 1, orders[i]) for i in range(2)]
    sums += [DpSum(up_half(g), width, 0, o) for g, o in zip((gate_grad, up_grad), orders)]
    for one in sums:
        one.begin()
    for one in sums:
        one.keep()
    branch_parts = [
        jnp.dot(hidden, w_down[:, i * cut : (i + 1) * cut], preferred_element_type=f32).astype(bf16)
        for i in range(2)
    ]
    for one in sums:
        one.fold()
        one.back()

    scatter_branch = lambda part: lax.psum_scatter(part, "tp", scatter_dimension=0, tiled=True)
    branch_parts = [tie(part, norm_grad) if i else part for i, part in enumerate(branch_parts)]
    branch = [scatter_branch(branch_parts[0])]

    norm_grad = tie(norm_grad, *[one.own for one in sums])
    back_two, grad_gain_mlp = norm_back(residual, inv_second, gain_mlp, norm_grad.astype(f32))
    resid_grad = upstream.astype(f32) + back_two
    out_low = resid_grad.astype(bf16)
    attended_grad = dot_t(out_low, w_out)
    out_sent = swap(x_t_y(mixed_other, tie(out_low, attended_grad)).astype(bf16), "tp", 0)
    for one in sums:
        one.back_more(attended_grad)
    back = []
    dy = tie(attended_grad, *[one.half for one in sums])
    for s in range(seq_count):
        back.append(
            attend_back(
                of_seq(q, s), of_seq(mixed_low, s), of_seq(dy, s), [of_seq(x, s) for x in kvs]
            )
        )
    dq = joined([x[0] for x in back])
    dks = [joined([x[1][b] for x in back]) for b in range(hops + 1)]
    dvs = [joined([x[2][b] for x in back]) for b in range(hops + 1)]
    come = window_sum(
        [jnp.concatenate([dv, dk.astype(bf16)], axis=1) for dv, dk in zip(dvs[1:], dks[1:])]
    )
    value_grad_low = (dvs[0] + come[:, :width]).astype(bf16)
    key_grad_low = (dks[0] + come[:, width:]).astype(bf16)
    query_grad_low = dq.astype(bf16)
    out_part = (x_t_y(mixed_mine, tie(out_low, dq)) + out_sent.astype(f32)).astype(bf16)
    out_halves = rows_over_dp(out_part)
    low = jnp.concatenate([value_grad_low, query_grad_low, key_grad_low], axis=1)
    low_sent = swap(x_t_y(first_other, low).astype(bf16), "tp", 0)
    low_part = (x_t_y(first_mine, low) + low_sent.astype(f32)).astype(bf16)
    low_halves = rows_over_dp(low_part)
    branch.append(scatter_branch(tie(branch_parts[1], low)))
    grad_w_out = rows_over_chips(out_halves)
    grads = rows_over_chips(low_halves)
    grad_w_value = grads[:, :width]
    grad_w_query = grads[:, width : width + narrow]
    grad_w_key = grads[:, width + narrow :]
    output = (residual + jnp.concatenate(branch, axis=1).astype(f32)).astype(bf16)
    output = output.reshape(tokens.shape)
    first_grad = jnp.einsum("nk,dk->nd", query_grad_low, w_query, preferred_element_type=f32)
    first_grad = first_grad + jnp.einsum(
        "nk,dk->nd", key_grad_low, w_key, preferred_element_type=f32
    )
    first_grad = first_grad + jnp.einsum(
        "nk,dk->nd", value_grad_low, w_value, preferred_element_type=f32
    )
    back_one, grad_gain_attn = norm_back(inputs, inv_first, gain_attn, first_grad)
    input_grad = (resid_grad + back_one).reshape(tokens.shape)
    gains = scatter_vectors(jnp.stack([grad_gain_attn, grad_gain_mlp]))
    late = lax.optimization_barrier((low_part,) + tuple(one.far for one in sums))
    for one, far in zip(sums, late[1:]):
        one.far = far
    ends = [one.end() for one in sums]
    grad_down = jnp.concatenate(ends[0] + ends[1], axis=1)
    grad_gate_up = jnp.stack([jnp.concatenate(x, axis=0) for x in ends[2:]])
    return (
        output,
        input_grad,
        gains[0],
        grad_w_query,
        grad_w_key,
        grad_w_value,
        grad_w_out,
        gains[1],
        grad_gate_up,
        grad_down,
    )


def solution(mesh):
    placed = (
        P("dp", "tp", None),
        P("dp", "tp"),
        P("dp"),
        P(),
        P(),
        P(),
        P(),
        P(),
        P(),
        P(None, None, "tp"),
        P("tp", None),
        P("dp", "tp", None),
    )
    return jax.shard_map(
        local,
        mesh=mesh,
        in_specs=placed,
        out_specs=(
            P("dp", "tp", None),
            P("dp", "tp", None),
            P(("dp", "tp")),
            P(("dp", "tp"), None),
            P(("dp", "tp"), None),
            P(("dp", "tp"), None),
            P(("dp", "tp"), None),
            P(("dp", "tp")),
            P(None, None, "tp"),
            P("tp", None),
        ),
        check_vma=False,
    )
```
